256 devices in a mesh: space: 16 (over z, core), tm: 16 (over x, y).
Axes of the slice: x: 4, y: 4, z: 8, core: 2. Of those that a mesh axis runs over, the one named last changes fastest.
Arguments:
- velocity: bfloat16 [3, 128, 128, 8192], P(None, 'tm', 'space'), may hold values from -12 to 12, as said below
- metrics: bfloat16 [5, 128, 8192], P(None, 'space'), may hold values from 0.25 to 2
- basis: bfloat16 [32, 3, 128, 8192], P(None, None, 'space'), may hold values from -0.0034179688 to 0.0034179688
Outputs:
- coefficients: float32 [128, 32], P('tm')
- rfactor: float32 [128, 8], P('tm')
- window: float32 [512, 32], P('tm')
The draws below stay inside these ranges and needn't reach their ends.
Inputs may be any that keep to these rules, and one draw needn't show every extreme that they name: `velocity`: entries are real velocities of order one.
All inputs are finite; a program needn't handle non-finite values.
Results may differ from the reference program's by a relative error of at most 0.0029.
Values may be sent and summed in bfloat16 or wider, within the bound.
A program may use at most 192 MiB of HBM per device.

```python
import jax
import jax.numpy as jnp
from jax import lax

NY = 128
NZ = 64
SNAP = 8
RANK = 32
NX = 128
SNAPS = 128
N_TM = 16


def draw_velocity(key, part):
    mixing_fields = 64
    key_fields = jax.random.fold_in(key, 21)
    key_weights = jax.random.fold_in(key, 23)
    key_own = jax.random.fold_in(key, 25)
    key_amp = jax.random.fold_in(key, 26)
    cells = NY * NZ
    fields = jax.random.randint(key_fields, (mixing_fields, 3, NX, cells), -128, 129, dtype=jnp.int32)
    weights = jax.random.randint(key_weights, (SNAPS, mixing_fields), -4, 5, dtype=jnp.int32)
    amp = jax.random.randint(key_amp, (1, SNAPS, 1, 1), 2, 7, dtype=jnp.int32)
    own = jax.random.randint(key_own, (3, SNAPS, NX, cells), -128, 129, dtype=jnp.int32).astype(jnp.float32)
    mixed = jnp.einsum('sk,kcxm->csxm', weights.astype(jnp.float32), fields.astype(jnp.float32), precision=lax.Precision.HIGHEST)
    values = amp.astype(jnp.float32) * (mixed + 12.0 * own) / 4096.0
    return jnp.clip(values, -12.0, 12.0).astype(jnp.bfloat16)


def block_levels(key, extent, cuts, least, high):
    def one(dim, parts):
        draws = jax.random.uniform(jax.random.fold_in(jax.random.fold_in(key, 6), dim), (parts,), jnp.float32, least / len(cuts), high / len(cuts))
        return jnp.repeat(jnp.exp(draws), extent[dim] // parts).reshape((-1,) + (1,) * (len(extent) - dim - 1))

    gain = one(*cuts[0])
    for cut in cuts[1:]:
        gain = gain * one(*cut)
    return gain


def normal_values(stream_key, dims, spread, most, pieces=(), kind=jnp.bfloat16):
    array = jax.random.normal(stream_key, dims, jnp.float32) * spread
    if len(pieces) > 0:
        array = block_levels(stream_key, dims, pieces, -0.22, 0.18) * array
    return jnp.clip(array, min=-most, max=most).astype(kind)


def setup_inputs(seed: int = 0) -> dict:
    key_of = jax.random.split(jax.random.key(seed), 4)
    return {
        "velocity": draw_velocity(jax.random.fold_in(key_of[3], 71), 0),
        "metrics": jnp.clip(0.25 + 1.75 * jax.random.uniform(key_of[1], (5, NX, NY * NZ), jnp.float32) ** block_levels(key_of[1], (5, NX, NY * NZ), ((1, 16),), -0.2, 0.2), 0.25, 2.0).astype(jnp.bfloat16),
        "basis": normal_values(key_of[2], (RANK, 3, NX, NY * NZ), (3 * NX * NY * NZ) ** -0.5, 0.0034179688, ((2, 16),)),
    }


def vorticity_of(padded, metrics):
    field = padded.astype(jnp.float32)
    coeffs = metrics.astype(jnp.float32)
    dxi = (field[:, :, 2:] - field[:, :, :-2]) * 0.5
    inner = field[:, :, 1:-1]
    width = inner.shape[-1]
    zeros = jnp.zeros(inner.shape[:-1] + (NZ,), jnp.float32)
    upper = jnp.concatenate([inner[..., NZ:], zeros], -1)
    lower = jnp.concatenate([zeros, inner[..., :-NZ]], -1)
    deta = (upper - lower) * 0.5
    column = jnp.arange(width, dtype=jnp.int32) % NZ
    plus = jnp.where(column == NZ - 1, jnp.roll(inner, NZ - 1, -1), jnp.roll(inner, -1, -1))
    minus = jnp.where(column == 0, jnp.roll(inner, -(NZ - 1), -1), jnp.roll(inner, 1, -1))
    dzeta = (plus - minus) * 0.5
    xi_x = coeffs[0][None]
    eta_x = coeffs[1][None]
    xi_y = coeffs[2][None]
    eta_y = coeffs[3][None]
    zeta_z = coeffs[4][None]

    def ddx(comp):
        return xi_x * dxi[comp] + eta_x * deta[comp]

    def ddy(comp):
        return xi_y * dxi[comp] + eta_y * deta[comp]

    def ddz(comp):
        return zeta_z * dzeta[comp]
    first = ddy(2) - ddz(1)
    second = ddz(0) - ddx(2)
    third = ddx(1) - ddy(0)
    return jnp.stack([first, second, third]).astype(jnp.bfloat16)

def reference(velocity, metrics, basis):
    groups = velocity.reshape(3, N_TM, SNAP, NX, NY * NZ)
    basis_wide = basis.astype(jnp.float32)
    rows_total = 3.0 * NX * NY * NZ

    def one_group(index):
        part = lax.dynamic_index_in_dim(groups, index, 1, keepdims=False)
        padded = jnp.concatenate([part[:, :, -1:], part, part[:, :, :1]], 2)
        vort = vorticity_of(padded, metrics).astype(jnp.float32)
        coeff = jnp.einsum('csxm,rcxm->sr', vort, basis_wide, precision=lax.Precision.HIGHEST)
        gram = jnp.einsum('csxm,ctxm->st', vort, vort, precision=lax.Precision.HIGHEST) / rows_total
        factor = jnp.linalg.cholesky(gram).T
        term = jnp.dot(coeff.T, coeff, precision=lax.Precision.HIGHEST) / SNAP
        return (coeff, factor, term)
    coeffs, factors, terms = lax.map(one_group, jnp.arange(N_TM, dtype=jnp.int32))
    window = jnp.cumsum(terms, 0)
    return (coeffs.reshape(SNAPS, RANK), factors.reshape(N_TM * SNAP, SNAP), window.reshape(N_TM * RANK, RANK))
```

```python
import functools

import jax
import jax.numpy as jnp
from jax import lax
from jax.experimental import pallas as pl
from jax.experimental.pallas import tpu as pltpu
from jax.sharding import PartitionSpec as P

NZ = 64
LANES = 128
CHUNK = 1024
HIGH = lax.Precision.HIGHEST
MESH = pl.DeviceIdType.MESH
F32 = jnp.float32
BF16 = jnp.bfloat16


def iota(shape, dim):
    return lax.broadcasted_iota(jnp.int32, shape, dim)


def kernel(n_sp, n_tm, snaps, rank, planes, rows_total,
           vel_hbm, met_hbm, bas_hbm,
           coef_ref, rfac_ref, win_ref,
           vel, met, bas, metf, out_lo, out_hi, in_lo, in_hi, half_lo, half_hi,
           vort, acc_b, acc_v, part, call,
           sem_v, sem_m, sem_b, sem_slo, sem_shi, sem_rlo, sem_rhi,
           sem_ps, sem_pr, sem_cs, sem_cr):
    sp = lax.axis_index("space")
    tm = lax.axis_index("tm")
    cells = met_hbm.shape[2]
    chunks = cells // CHUNK
    tiles = CHUNK // LANES
    rows = snaps * planes
    brows = rank * planes
    right = lax.rem(sp + 1, n_sp)
    left = lax.rem(sp + n_sp - 1, n_sp)

    barrier = pltpu.get_barrier_semaphore()

    def hello_sp(d, _):
        pl.semaphore_signal(barrier, inc=1, device_id=(lax.rem(sp + d, n_sp), tm), device_id_type=MESH)
        return 0

    def hello_tm(d, _):
        pl.semaphore_signal(barrier, inc=1, device_id=(sp, lax.rem(tm + d, n_tm)), device_id_type=MESH)
        return 0

    lax.fori_loop(1, n_sp, hello_sp, 0)
    lax.fori_loop(1, n_tm, hello_tm, 0)

    def at(k):
        return pl.ds(pl.multiple_of(k * CHUNK, CHUNK), CHUNK)

    def vel_at(k):
        return pl.ds(pl.multiple_of(k * CHUNK + LANES, LANES), CHUNK)

    def vel_copy(k):
        return pltpu.make_async_copy(vel_hbm.at[:, at(k)], vel.at[:, vel_at(k)], sem_v.at[k])

    def bas_copy(k):
        return pltpu.make_async_copy(bas_hbm.at[:, :, :, at(k)], bas.at[:, :, :, at(k)], sem_b.at[k])

    met_copy = pltpu.make_async_copy(met_hbm, met, sem_m)

    def start_vel(k, _):
        vel_copy(k).start()
        return 0

    def start_bas(k, _):
        bas_copy(k).start()
        return 0

    lax.fori_loop(0, chunks, start_vel, 0)
    met_copy.start()
    lax.fori_loop(0, chunks, start_bas, 0)

    zero_tile = jnp.zeros((vel.shape[0], LANES), BF16)
    vel[:, pl.ds(0, LANES)] = zero_tile
    vel[:, pl.ds(cells + LANES, LANES)] = zero_tile
    acc_b[...] = jnp.zeros_like(acc_b)
    acc_v[...] = jnp.zeros_like(acc_v)

    edge = 3 * snaps
    pick_row = iota((2 * edge, vel.shape[0]), 0)
    pick_col = iota((2 * edge, vel.shape[0]), 1)
    wanted = jnp.where(pick_row < edge, pick_row * planes, (pick_row - edge) * planes + planes - 1)
    pick = jnp.where(pick_col == wanted, 1.0, 0.0).astype(BF16)

    def lo_copy(k):
        return pltpu.make_async_remote_copy(
            src_ref=out_lo.at[:, at(k)], dst_ref=in_hi.at[:, at(k)],
            send_sem=sem_slo.at[k], recv_sem=sem_rhi.at[k],
            device_id=(left, tm), device_id_type=MESH)

    def hi_copy(k):
        return pltpu.make_async_remote_copy(
            src_ref=out_hi.at[:, at(k)], dst_ref=in_lo.at[:, at(k)],
            send_sem=sem_shi.at[k], recv_sem=sem_rlo.at[k],
            device_id=(right, tm), device_id_type=MESH)

    def extract(k, _):
        vel_copy(k).wait()
        got = jnp.dot(pick, vel[:, vel_at(k)], preferred_element_type=F32).astype(BF16)
        out_lo[:, at(k)] = got[:edge]
        out_hi[:, at(k)] = got[edge:]
        return 0

    lax.fori_loop(0, chunks, extract, 0)
    pl.semaphore_wait(barrier, n_sp - 1 + n_tm - 1)

    def send(k, _):
        lo_copy(k).start()
        hi_copy(k).start()
        return 0

    lax.fori_loop(0, chunks, send, 0)
    met_copy.wait()
    for i in range(5):
        def scale(k, _):
            metf[i, :, at(k)] = met[i, :, at(k)].astype(F32) * 0.5
            return 0
        lax.fori_loop(0, chunks, scale, 0)

    lane = iota((planes, LANES), 1)
    row = iota((planes, LANES), 0)
    low_half = lane < NZ
    first_k = lane % NZ == 0
    last_k = lane % NZ == NZ - 1
    first_x = row == 0
    last_x = row == planes - 1

    def chunk(k, _):
        lo_copy(k).wait()
        hi_copy(k).wait()
        half_lo[...] = in_lo[:, at(k)].astype(F32)
        half_hi[...] = in_hi[:, at(k)].astype(F32)
        base = k * CHUNK

        def load(c, s, t):
            where = pl.ds(pl.multiple_of(base + (t + 1) * LANES, LANES), LANES)
            return vel[pl.ds((c * snaps + s) * planes, planes), where].astype(F32)

        for pair in range(snaps // 2):
            prev = {}
            cur = {}
            curR = {}
            D = {}
            for s in (2 * pair, 2 * pair + 1):
                for c in range(3):
                    a = pltpu.roll(load(c, s, -1), NZ, 1)
                    cur[s, c] = load(c, s, 0)
                    curR[s, c] = pltpu.roll(cur[s, c], NZ, 1)
                    D[s, c] = curR[s, c] - a
            for t in range(tiles):
                mwhere = pl.ds(pl.multiple_of(base + t * LANES, LANES), LANES)
                xi_x, eta_x, xi_y, eta_y, zeta = (metf[i, :, mwhere] for i in range(5))
                res = []
                for s in (2 * pair, 2 * pair + 1):
                    dxi, deta, dz = [], [], []
                    for c in range(3):
                        f = cur[s, c]
                        R = curR[s, c]
                        nxt = load(c, s, t + 1)
                        nxtR = pltpu.roll(nxt, NZ, 1)
                        Dn = nxtR - R
                        deta.append(jnp.where(low_half, D[s, c], Dn))
                        if c < 2:
                            plus = pltpu.roll(jnp.where(first_k, R, f), LANES - 1, 1)
                            minus = pltpu.roll(jnp.where(last_k, R, f), 1, 1)
                            dz.append(plus - minus)
                        lo = jnp.broadcast_to(half_lo[pl.ds(c * snaps + s, 1), pl.ds(t * LANES, LANES)], (planes, LANES))
                        hi = jnp.broadcast_to(half_hi[pl.ds(c * snaps + s, 1), pl.ds(t * LANES, LANES)], (planes, LANES))
                        xp = pltpu.roll(jnp.where(first_x, hi, f), planes - 1, 0)
                        xm = pltpu.roll(jnp.where(last_x, lo, f), 1, 0)
                        dxi.append(xp - xm)
                        cur[s, c], curR[s, c], D[s, c] = nxt, nxtR, Dn
                    one = xi_y * dxi[2] + eta_y * deta[2] - zeta * dz[1]
                    two = zeta * dz[0] - (xi_x * dxi[2] + eta_x * deta[2])
                    three = (xi_x * dxi[1] + eta_x * deta[1]) - (xi_y * dxi[0] + eta_y * deta[0])
                    res.append((one, two, three))
                for c in range(3):
                    both = jnp.concatenate([res[0][c], res[1][c]], axis=0).astype(BF16)
                    vort[c, pl.ds(2 * pair * planes, 2 * planes), pl.ds(t * LANES, LANES)] = both
        bas_copy(k).wait()
        nt = (((1,), (1,)), ((), ()))
        for c in range(3):
            v = vort[c]
            b = bas[:, c, :, at(k)].reshape(brows, CHUNK)
            acc_b[...] += lax.dot_general(v, b, nt, preferred_element_type=F32)
            acc_v[...] += lax.dot_general(v, v, nt, preferred_element_type=F32)
        return 0

    lax.fori_loop(0, chunks, chunk, 0)

    def keep_same(acc):
        same = iota(acc.shape, 0) % planes == iota(acc.shape, 1) % planes
        return jnp.where(same, acc[...], 0.0)

    def gather_to(count, first):
        src = iota((count, LANES), 0) // planes + first
        return jnp.where(src == iota((count, LANES), 1), 1.0, 0.0)

    wide = (jnp.dot(keep_same(acc_b), gather_to(brows, 0), preferred_element_type=F32, precision=HIGH)
            + jnp.dot(keep_same(acc_v), gather_to(rows, rank), preferred_element_type=F32, precision=HIGH))
    part[sp] = jnp.sum(wide.reshape(snaps, planes, LANES), axis=1)

    def part_copy(d):
        return pltpu.make_async_remote_copy(
            src_ref=part.at[sp], dst_ref=part.at[sp],
            send_sem=sem_ps.at[d], recv_sem=sem_pr.at[sp],
            device_id=(lax.rem(sp + d, n_sp), tm), device_id_type=MESH)

    def part_arrival(d):
        src = lax.rem(sp + d, n_sp)
        return pltpu.make_async_remote_copy(
            src_ref=part.at[src], dst_ref=part.at[src],
            send_sem=sem_ps.at[d], recv_sem=sem_pr.at[src],
            device_id=(src, tm), device_id_type=MESH)

    def part_start(d, _):
        part_copy(d).start()
        return 0

    def part_wait(d, _):
        part_arrival(d).wait_recv()
        return 0

    lax.fori_loop(1, n_sp, part_start, 0)
    lax.fori_loop(1, n_sp, part_wait, 0)
    total = jnp.sum(part[...], axis=0)
    wlane = iota((snaps, LANES), 1)
    call[tm] = jnp.where(wlane < rank, total, 0.0)

    def call_copy(d):
        return pltpu.make_async_remote_copy(
            src_ref=call.at[tm], dst_ref=call.at[tm],
            send_sem=sem_cs.at[d], recv_sem=sem_cr.at[tm],
            device_id=(sp, lax.rem(tm + d, n_tm)), device_id_type=MESH)

    def call_arrival(d):
        src = lax.rem(tm + d, n_tm)
        return pltpu.make_async_remote_copy(
            src_ref=call.at[src], dst_ref=call.at[src],
            send_sem=sem_cs.at[d], recv_sem=sem_cr.at[src],
            device_id=(sp, src), device_id_type=MESH)

    def call_start(d, _):
        call_copy(d).start()
        return 0

    def call_wait(d, _):
        call_arrival(d).wait_recv()
        return 0

    lax.fori_loop(1, n_tm, call_start, 0)

    coef_ref[...] = total[:, :rank]
    left_edge = pltpu.roll(total, LANES - rank, 1)
    a = jnp.where(wlane < snaps, left_edge, 0.0) / rows_total
    u_rows = []
    for j in range(snaps):
        d = a[j:j + 1, j:j + 1]
        line = a[j:j + 1, :]
        u_rows.append(jnp.where(iota((1, LANES), 1) >= j, line * lax.rsqrt(d), 0.0))
        if j < snaps - 1:
            a = a - (a[:, j:j + 1] / d) * line
    rfac_ref[...] = jnp.concatenate(u_rows, axis=0)[:, :snaps]

    lax.fori_loop(1, n_tm, call_wait, 0)
    every = call[...].reshape(n_tm * snaps, LANES)
    every = jnp.where(iota(every.shape, 0) < (tm + 1) * snaps, every, 0.0)
    win = lax.dot_general(every, every, (((0,), (0,)), ((), ())), preferred_element_type=F32, precision=HIGH)
    win_ref[...] = win[:rank, :rank] / snaps

    def part_end(d, _):
        part_copy(d).wait_send()
        return 0

    def call_end(d, _):
        call_copy(d).wait_send()
        return 0

    lax.fori_loop(1, n_sp, part_end, 0)
    lax.fori_loop(1, n_tm, call_end, 0)


def on_device(velocity, metrics, basis):
    n_sp = lax.axis_size("space")
    n_tm = lax.axis_size("tm")
    comps, snaps, planes, cells = velocity.shape
    rank = basis.shape[0]
    rows_total = float(3 * planes * n_sp * cells)
    chunks = cells // CHUNK
    vrows = comps * snaps * planes
    edge = comps * snaps
    anywhere = pl.BlockSpec(memory_space=pl.ANY)
    inside = pl.BlockSpec(memory_space=pltpu.VMEM)
    dma = pltpu.SemaphoreType.DMA
    return pl.pallas_call(
        functools.partial(kernel, n_sp, n_tm, snaps, rank, planes, rows_total),
        out_shape=(
            jax.ShapeDtypeStruct((snaps, rank), F32),
            jax.ShapeDtypeStruct((snaps, snaps), F32),
            jax.ShapeDtypeStruct((rank, rank), F32),
        ),
        in_specs=[anywhere] * 3,
        out_specs=(inside,) * 3,
        scratch_shapes=[
            pltpu.VMEM((vrows, cells + 2 * LANES), BF16),
            pltpu.VMEM(metrics.shape, BF16),
            pltpu.VMEM(basis.shape, BF16),
            pltpu.VMEM(metrics.shape, F32),
            pltpu.VMEM((edge, cells), BF16),
            pltpu.VMEM((edge, cells), BF16),
            pltpu.VMEM((edge, cells), BF16),
            pltpu.VMEM((edge, cells), BF16),
            pltpu.VMEM((edge, CHUNK), F32),
            pltpu.VMEM((edge, CHUNK), F32),
            pltpu.VMEM((comps, snaps * planes, CHUNK), BF16),
            pltpu.VMEM((snaps * planes, rank * planes), F32),
            pltpu.VMEM((snaps * planes, snaps * planes), F32),
            pltpu.VMEM((n_sp, snaps, LANES), F32),
            pltpu.VMEM((n_tm, snaps, LANES), F32),
            dma((chunks,)), dma(()), dma((chunks,)),
            dma((chunks,)), dma((chunks,)), dma((chunks,)), dma((chunks,)),
            dma((n_sp,)), dma((n_sp,)), dma((n_tm,)), dma((n_tm,)),
        ],
        compiler_params=pltpu.CompilerParams(collective_id=0, has_side_effects=True),
    )(velocity.reshape(vrows, cells), metrics, basis)


def solution(mesh):
    return jax.shard_map(
        on_device,
        mesh=mesh,
        in_specs=(
            P(None, "tm", "space", None),
            P(None, "space", None),
            P(None, None, "space", None),
        ),
        out_specs=(P("tm", None), P("tm", None), P("tm", None)),
        check_vma=False,
    )
```
